256 devices in a mesh: ctx: 16 (over z, x_lo), uly: 16 (over x_hi, y, core).
Axes of the slice: x: 4 (x_hi: 2, x_lo: 2; x = x_hi * 2 + x_lo), y: 4, z: 8, core: 2. Of those that a mesh axis runs over, the one named last changes fastest.
Arguments:
- q_new: bfloat16 [4096, 4096], P(('ctx', 'uly')), may hold values from -20 to 20
- k_new: bfloat16 [4096, 4096], P(('ctx', 'uly')), may hold values from -6 to 6
- v_new: bfloat16 [4096, 4096], P(('ctx', 'uly')), may hold values from -6 to 6
- cache_k: bfloat16 [16384, 4096], P('ctx', 'uly'), may hold values from -4 to 4
- cache_v: bfloat16 [16384, 4096], P('ctx', 'uly'), may hold values from -6 to 6
- filled_slots: int32 [1], replicated, may hold values from 8193 to 16384
- norm_gain: float32 [4096], replicated, may hold values from 0.1 to 1.9
- v_branch: bfloat16 [4096, 4096], P(('ctx', 'uly')), may hold values from -6 to 6
- x_gate: bfloat16 [4096, 4096], P(('ctx', 'uly')), may hold values from -6 to 6
- conv_state: bfloat16 [6, 4096], replicated, may hold values from -6 to 6
- conv_filter: float32 [7, 256], replicated, may hold values from -2 to 2
- skip_gain: float32 [4096], replicated, may hold values from -1 to 1
Outputs:
- mixed: bfloat16 [4096, 4096], P(('ctx', 'uly'))
The draws below stay inside these ranges and needn't reach their ends.
All inputs are finite; a program needn't handle non-finite values.
Results may differ from the reference program's by a relative error of at most 0.04.
Values may be sent and summed in bfloat16 or wider, within the bound.
A program may use at most 64 MiB of HBM per device.

```python
import math
import jax
import jax.numpy as jnp
from jax import lax

D = 4096
HEADS = 32
DH = 128
CHAN_GROUP = 16
TAPS = 7
TOKENS = 4096
CACHE = 16384
GROUPS = 256


def draw_q_new(key, part):
    base = jnp.clip(jax.random.normal(jax.random.fold_in(key, 11), (TOKENS, HEADS * DH), jnp.float32), -4.0, 4.0)
    return base.astype(jnp.bfloat16)


def draw_cache_k(key, part):
    base = jnp.clip(jax.random.normal(jax.random.fold_in(key, 21), (CACHE, HEADS * DH), jnp.float32), -4.0, 4.0)
    return base.astype(jnp.bfloat16)


def shard_levels(stream_key, dims, split, least, high):
    def one(axis_at, blocks):
        draws = jax.random.uniform(jax.random.fold_in(jax.random.fold_in(stream_key, 6), axis_at), (blocks,), jnp.float32, least / len(split), high / len(split))
        return jnp.repeat(jnp.exp(draws), dims[axis_at] // blocks).reshape((-1,) + (1,) * (len(dims) - axis_at - 1))

    level = one(*split[0])
    for cut in split[1:]:
        level = level * one(*cut)
    return level


def bell_draw(rng, dims, deviation, limit, pieces=(), kind=jnp.bfloat16):
    entries = deviation * jax.random.normal(rng, dims, jnp.float32)
    if pieces:
        entries = entries * shard_levels(rng, dims, pieces, -0.22, 0.18)
    return jnp.clip(entries, -limit, limit).astype(kind)


def setup_inputs(seed: int = 0) -> dict:
    splits = jax.random.split(jax.random.key(seed), 13)
    return {
        "q_new": draw_q_new(jax.random.fold_in(splits[12], 71), 0),
        "k_new": bell_draw(splits[1], (TOKENS, D), 1.0, 6.0, ((0, 256),)),
        "v_new": bell_draw(splits[2], (TOKENS, D), 1.0, 6.0, ((0, 256),)),
        "cache_k": draw_cache_k(jax.random.fold_in(splits[12], 71), 0),
        "cache_v": bell_draw(splits[4], (CACHE, D), 1.0, 6.0, ((0, 16), (1, 16))),
        "filled_slots": jax.random.randint(splits[5], (1,), CACHE // 2 + 1, CACHE + 1).astype(jnp.int32),
        "norm_gain": jnp.clip(1.0 + 0.18 * jax.random.normal(splits[6], (D,), jnp.float32), 0.1, 1.9),
        "v_branch": bell_draw(splits[7], (TOKENS, D), 1.0, 6.0, ((0, 256),)),
        "x_gate": bell_draw(splits[8], (TOKENS, D), 1.0, 6.0, ((0, 256),)),
        "conv_state": bell_draw(splits[9], (TAPS - 1, D), 1.0, 6.0),
        "conv_filter": bell_draw(splits[10], (TAPS, GROUPS), TAPS ** -0.5, 2.0, (), jnp.float32),
        "skip_gain": jnp.clip(jax.random.uniform(splits[11], (D,), jnp.float32, -1.0, 1.0), -1.0, 1.0),
    }


def reference(q_new, k_new, v_new, cache_k, cache_v, filled_slots, norm_gain, v_branch, x_gate, conv_state, conv_filter, skip_gain):
    cache_limit = filled_slots[0]
    all_keys = jnp.concatenate([cache_k, k_new], axis=0)
    all_values = jnp.concatenate([cache_v, v_new], axis=0)
    slot_ids = jnp.arange(all_keys.shape[0], dtype=jnp.int32)[None, :]
    score_scale = 1.0 / math.sqrt(DH)
    block_width = math.gcd(TOKENS, 1024)
    block_count = TOKENS // block_width

    def one_head(head_id):
        head_q = lax.dynamic_slice_in_dim(q_new, head_id * DH, DH, 1)
        head_k = lax.dynamic_slice_in_dim(all_keys, head_id * DH, DH, 1)
        head_v = lax.dynamic_slice_in_dim(all_values, head_id * DH, DH, 1)

        def one_block(block_id):
            queries = lax.dynamic_slice_in_dim(head_q, block_id * block_width, block_width, 0)
            positions = (block_id * block_width + jnp.arange(block_width, dtype=jnp.int32))[:, None]
            scores = jnp.dot(queries, head_k.T, preferred_element_type=jnp.float32) * score_scale
            valid_mask = jnp.where(slot_ids < CACHE, slot_ids < cache_limit, slot_ids - CACHE <= positions)
            scores = jnp.where(valid_mask, scores, -jnp.inf)
            largest = lax.optimization_barrier(jnp.max(scores, axis=1, keepdims=True))
            weights = jnp.exp(scores - largest)
            denominator = lax.optimization_barrier(jnp.sum(weights, axis=1, keepdims=True))
            numerator = jnp.dot(weights.astype(jnp.bfloat16), head_v, preferred_element_type=jnp.float32)
            return numerator / denominator
        return lax.map(one_block, jnp.arange(block_count, dtype=jnp.int32)).reshape(TOKENS, DH)
    per_head = lax.map(one_head, jnp.arange(HEADS, dtype=jnp.int32))
    attended = jnp.transpose(per_head, (1, 0, 2)).reshape(TOKENS, D).astype(jnp.bfloat16)
    values32 = attended.astype(jnp.float32)
    normed = values32 * lax.rsqrt(lax.optimization_barrier(jnp.mean(values32 * values32, axis=1, keepdims=True)) + 1e-06) * norm_gain
    conv_input = lax.optimization_barrier((normed * v_branch.astype(jnp.float32)).astype(jnp.bfloat16))
    extended = jnp.concatenate([conv_state, conv_input], axis=0).astype(jnp.float32)
    tap_table = jnp.repeat(conv_filter, CHAN_GROUP, axis=1)
    conv_reach = TAPS - 1
    filtered = tap_table[0] * extended[conv_reach:conv_reach + TOKENS]
    for shift_lag in range(1, TAPS):
        filtered = filtered + tap_table[shift_lag] * extended[conv_reach - shift_lag:conv_reach - shift_lag + TOKENS]
    result = x_gate.astype(jnp.float32) * (filtered + skip_gain * conv_input.astype(jnp.float32))
    return result.astype(jnp.bfloat16)
```

```python
import functools
import math

import jax
import jax.numpy as jnp
from jax import lax
from jax.experimental import pallas as pl
from jax.experimental.pallas import tpu as pltpu
from jax.sharding import PartitionSpec as P

MESH = pl.DeviceIdType.MESH
DH = 128
FLAG_ROWS = 16
NEG = -1e30
BIG = 1e30
BF = jnp.bfloat16
F32 = jnp.float32


def nt(a, b):
    return lax.dot_general(a, b, (((1,), (1,)), ((), ())), preferred_element_type=F32)


def kernel(
    Z, U, filled,
    q, k, v, ck, cv, gain, vb, xg, cstate, taps, skip,
    out,
    qbuf, kvn, raw, ka, kb, va, vt_b, o_a, m_a, o_s, o_r, s_s, s_r, obuf, att, hs, hr, ext,
    own_sem, x_send, x_recv, q_send, q_recv, n_send, n_recv,
    g_send, g_recv, r_send, r_recv, t_send, t_recv, b_send, b_recv, h_send, h_recv,
):
    T, D = q.shape
    S = ck.shape[0]
    W = 2 * U
    R = U * T
    H = Z // 2
    c_i = lax.axis_index("ctx")
    u = lax.axis_index("uly")
    z, xl = c_i // 2, lax.rem(c_i, 2)
    me = xl * U + u
    head_col = pl.multiple_of((2 * u + xl) * DH, DH)
    scale = math.log2(math.e) / math.sqrt(DH)

    def peer(o):
        return (2 * z + o // U, lax.rem(o, U))

    def ring(d):
        return lax.rem(z + Z + d, Z)

    partner = (2 * z + 1 - xl, u)
    flat = c_i * U + u
    n_dev = 2 * Z * U
    after, before = lax.rem(flat + 1, n_dev), lax.rem(flat + n_dev - 1, n_dev)

    barrier = pltpu.get_barrier_semaphore()

    def greet(i, carry):
        pl.semaphore_signal(barrier, inc=1, device_id=peer(lax.rem(me + i, W)), device_id_type=MESH)
        return carry

    lax.fori_loop(1, W, greet, 0)
    for d in (1, -1):
        pl.semaphore_signal(barrier, inc=1, device_id=(2 * ring(d) + xl, u), device_id_type=MESH)
    for f in (after, before):
        pl.semaphore_signal(barrier, inc=1, device_id=(f // U, lax.rem(f, U)), device_id_type=MESH)

    mine = pl.multiple_of(xl * DH, DH)
    other = pl.multiple_of((1 - xl) * DH, DH)
    loads = [
        pltpu.make_async_copy(src.at[:, pl.ds(mine, DH)], raw.at[0, i], own_sem.at[i])
        for i, src in enumerate((ck, cv))
    ]
    for load in loads:
        load.start()
    pl.semaphore_wait(barrier, W + 3)

    my_rows = pl.ds(pl.multiple_of(me * T, T), T)

    def q_copy(o):
        ou, ox = lax.rem(o, U), o // U
        cols = pl.ds(pl.multiple_of((2 * ou + ox) * DH, DH), DH)
        return pltpu.make_async_remote_copy(
            q.at[:, cols], qbuf.at[z, my_rows], q_send, q_recv, device_id=peer(o), device_id_type=MESH
        )

    def n_copy(o, i):
        ou, ox = lax.rem(o, U), o // U
        cols = pl.ds(pl.multiple_of((2 * ou + ox) * DH, DH), DH)
        return pltpu.make_async_remote_copy(
            (k, v)[i].at[:, cols], kvn.at[i, my_rows], n_send, n_recv, device_id=peer(o), device_id_type=MESH
        )

    def send_q(i, carry):
        q_copy(lax.rem(me + i, W)).start()
        return carry

    def send_n(i, carry):
        o = lax.rem(me + i, W)
        n_copy(o, 0).start()
        n_copy(o, 1).start()
        return carry

    lax.fori_loop(1, W, send_q, 0)
    lax.fori_loop(1, W, send_n, 0)
    swaps = [
        pltpu.make_async_remote_copy(
            src.at[:, pl.ds(other, DH)], raw.at[1, i], x_send.at[i], x_recv.at[i],
            device_id=partner, device_id_type=MESH,
        )
        for i, src in enumerate((ck, cv))
    ]
    for swap in swaps:
        swap.start()
    qbuf[z, my_rows, :] = q[:, pl.ds(head_col, DH)]
    kvn[0, my_rows, :] = k[:, pl.ds(head_col, DH)]
    kvn[1, my_rows, :] = v[:, pl.ds(head_col, DH)]

    def split_store(dst, at, x):
        x = x * scale
        hi = x.astype(BF)
        dst[pl.ds(at, x.shape[0]), 0:DH] = hi
        dst[pl.ds(at, x.shape[0]), DH : 2 * DH] = (x - hi.astype(F32)).astype(BF)

    def prepare(which, chunk_ctx, kdst, vdst):
        limit = filled[0] - chunk_ctx * S
        rows = lax.broadcasted_iota(jnp.int32, (S, DH), 0)
        keys = raw[which, 0].astype(F32)
        first = keys[0:1]
        split_store(kdst, 0, jnp.where(rows < limit, keys, first))
        values = jnp.where(rows < limit, raw[which, 1].astype(F32), 0.0)
        vdst[0:DH, 0:S] = values.T.astype(BF)
        lane = lax.broadcasted_iota(jnp.int32, (FLAG_ROWS, S), 1)
        row = lax.broadcasted_iota(jnp.int32, (FLAG_ROWS, S), 0)
        vdst[DH : DH + FLAG_ROWS, 0:S] = jnp.where((row == 0) & (lane < limit), 1.0, 0.0).astype(BF)

    def prepare_new():
        split_store(kb, S, kvn[0].astype(F32))
        vt_b[0:DH, S : S + 2 * R] = kvn[1].astype(F32).T.astype(BF)
        row = lax.broadcasted_iota(jnp.int32, (FLAG_ROWS, 2 * R), 0)
        vt_b[DH : DH + FLAG_ROWS, S : S + 2 * R] = jnp.where(row == 0, 1.0, 0.0).astype(BF)

    for load in loads:
        load.wait()
    prepare(0, c_i, ka, va)

    def twice(zq, half):
        x = qbuf[zq, pl.ds(pl.multiple_of(half * R, R), R), :]
        return jnp.concatenate([x, x], axis=1)

    def has_slots(chunk_ctx):
        return jnp.broadcast_to(filled[0] - chunk_ctx * S, (1, R)) > 0

    def first_part(zq, half):
        s = nt(ka[...], twice(zq, half))
        top = jnp.max(s, axis=0, keepdims=True)
        p = jnp.exp2(s - top).astype(BF)
        o_a[zq, half] = jnp.dot(va[...], p, preferred_element_type=F32)
        m_a[zq, half] = jnp.where(has_slots(c_i), top, NEG)

    def q_hop(way, dist, half, zq):
        rows = pl.ds(pl.multiple_of(half * R, R), R)
        return pltpu.make_async_remote_copy(
            qbuf.at[zq, rows], qbuf.at[zq, rows], g_send.at[way, dist, half], g_recv.at[way, dist, half],
            device_id=(2 * ring(1 - 2 * way) + xl, u), device_id_type=MESH,
        )

    everyone = pl.ds(0, (W - 1) * T)
    pltpu.make_async_copy(qbuf.at[z, everyone], qbuf.at[z, everyone], q_recv).wait()
    for half in (0, 1):
        for way in (0, 1):
            q_hop(way, 0, half, z).start()

    steps = 2 * Z

    def place(t, t_near, t_far):
        j = lax.rem(t - 2, 4)
        return lax.rem(j, 2), (t - 2) // 4, j // 2

    def gather_step(t, carry):
        last = t >= steps - 2
        early = t < 2
        j = lax.rem(t + 2, 4)
        way = jnp.where(early, 0, jnp.where(last, t - (steps - 2), lax.rem(j, 2)))
        half = jnp.where(early, t, jnp.where(last, t - (steps - 2), j // 2))
        dist = (t + 2) // 4
        dist = jnp.where(last, H, jnp.where(early, 0, dist))
        zq = ring(dist * (2 * way - 1))

        @pl.when(t >= 2)
        def _():
            q_hop(way, dist - 1, half, zq).wait_recv()

            @pl.when((dist < H - 1) | ((dist == H - 1) & (half == way)))
            def _():
                q_hop(way, dist, half, zq).start()

        @pl.when(t == 3)
        def _():
            pltpu.make_async_copy(kvn.at[:, everyone], kvn.at[:, everyone], n_recv).wait()
            prepare_new()

        @pl.when(t == steps - 2)
        def _():
            for swap in swaps:
                swap.wait_recv()
            prepare(1, 2 * z + 1 - xl, kb, vt_b)

        first_part(zq, half)
        return carry

    lax.fori_loop(0, steps, gather_step, 0)

    def second_part(zq, half):
        s = nt(kb[...], twice(zq, half))
        s_c, s_n = s[0:S], s[S : S + 2 * R]
        key_at = z * (2 * R) + lax.broadcasted_iota(jnp.int32, (2 * R, R), 0)
        token_at = zq * (2 * R) + half * R + lax.broadcasted_iota(jnp.int32, (2 * R, R), 1)
        s_n = jnp.where(key_at <= token_at, s_n, NEG)
        filled_here = has_slots(2 * z + 1 - xl)
        top_c = jnp.where(filled_here, jnp.max(s_c, axis=0, keepdims=True), NEG)
        m_1 = m_a[zq, half]
        top = jnp.maximum(jnp.maximum(top_c, m_1), jnp.max(s_n, axis=0, keepdims=True))
        p_c = jnp.exp2(s_c - jnp.where(filled_here, top, BIG)).astype(BF)
        p_n = jnp.exp2(s_n - top).astype(BF)
        o = o_a[zq, half] * jnp.exp2(m_1 - top)
        o = o + jnp.dot(vt_b[...], jnp.concatenate([p_c, p_n], axis=0), preferred_element_type=F32)
        o_a[zq, half] = o
        m_a[zq, half] = top

    def o_hop(way, slot, half):
        to = (2 * ring(1 - 2 * way) + xl, u)
        return (
            pltpu.make_async_remote_copy(
                o_s.at[way, slot, half], o_r.at[way, slot, half], r_send.at[way, slot, half],
                r_recv.at[way, slot, half], device_id=to, device_id_type=MESH,
            ),
            pltpu.make_async_remote_copy(
                s_s.at[way, slot, half], s_r.at[way, slot, half], t_send.at[way, slot, half],
                t_recv.at[way, slot, half], device_id=to, device_id_type=MESH,
            ),
        )

    def merge(zq, half, way, slot):
        for hop in o_hop(way, slot, half):
            hop.wait_recv()
        m_1 = m_a[zq, half]
        m_2 = s_r[way, slot, half, 0:1]
        top = jnp.maximum(m_1, m_2)
        f_1, f_2 = jnp.exp2(m_1 - top), jnp.exp2(m_2 - top)
        m_a[zq, half] = top
        o_a[zq, half, 0:DH] = o_a[zq, half, 0:DH] * f_1 + o_r[way, slot, half].astype(F32) * f_2
        o_a[zq, half, DH : DH + 1] = o_a[zq, half, DH : DH + 1] * f_1 + s_r[way, slot, half, 1:2] * f_2

    def back(o, half_rows):
        return pltpu.make_async_remote_copy(
            obuf.at[pl.ds(pl.multiple_of(o * T, T), T)], att.at[:, pl.ds(head_col, DH)], b_send, b_recv,
            device_id=peer(o), device_id_type=MESH,
        )

    def scatter_step(t, carry):
        first = t < 2
        own = t >= steps - 2
        j = lax.rem(t + 2, 4)
        way = jnp.where(first, t, lax.rem(j, 2))
        half = jnp.where(first, t, jnp.where(own, t - (steps - 2), j // 2))
        dist = H - (t + 2) // 4
        dist = jnp.where(first, H, jnp.where(own, 0, dist))
        zq = ring(dist * (1 - 2 * way))
        second_part(zq, half)

        @pl.when(jnp.logical_not(own))
        def _():
            @pl.when((dist < H - 1) | ((dist == H - 1) & (half == way)))
            def _():
                merge(zq, half, way, dist)

            slot = dist - 1
            o_s[way, slot, half] = o_a[zq, half, 0:DH].astype(BF)
            s_s[way, slot, half, 0:1] = m_a[zq, half]
            s_s[way, slot, half, 1:2] = o_a[zq, half, DH : DH + 1]
            for hop in o_hop(way, slot, half):
                hop.start()

        @pl.when(own)
        def _():
            merge(z, half, 0, 0)
            merge(z, half, 1, 0)
            done = o_a[z, half, 0:DH] / o_a[z, half, DH : DH + 1]
            obuf[pl.ds(pl.multiple_of(half * R, R), R), :] = done.T.astype(BF)

            def send_back(i, c):
                o = half * U + lax.rem(u + i, U)

                @pl.when(o != me)
                def _():
                    back(o, None).start()

                return c

            lax.fori_loop(0, U, send_back, 0)

        return carry

    lax.fori_loop(0, steps, scatter_step, 0)

    att[:, pl.ds(head_col, DH)] = obuf[my_rows, :]

    pltpu.make_async_copy(qbuf.at[z, everyone], qbuf.at[z, everyone], q_send).wait()
    pltpu.make_async_copy(kvn.at[:, everyone], kvn.at[:, everyone], n_send).wait()
    for swap in swaps:
        swap.wait_send()
    for way in (0, 1):
        for half in (0, 1):
            for d in range(H):
                if d < H - 1 or half == way:
                    q_hop(way, d, half, z).wait_send()
                    for hop in o_hop(way, d, half):
                        hop.wait_send()
    others = pl.ds(0, (W - 1) * DH)
    pltpu.make_async_copy(att.at[:, others], att.at[:, others], b_recv).wait()
    pltpu.make_async_copy(att.at[:, others], att.at[:, others], b_send).wait()

    x = att[...].astype(F32)
    inv = lax.rsqrt(jnp.mean(x * x, axis=1, keepdims=True) + 1e-06)
    conv_in = (x * inv * gain[...] * vb[...].astype(F32)).astype(BF)
    mine_32 = conv_in.astype(F32)
    ext[8:24, :] = mine_32
    hs[...] = mine_32[T - 8 : T].astype(BF)
    halo = pltpu.make_async_remote_copy(
        hs, hr, h_send, h_recv, device_id=(after // U, lax.rem(after, U)), device_id_type=MESH
    )
    halo.start()
    halo.wait()
    ext[0:8, :] = jnp.where(flat == 0, cstate[...].astype(F32), hr[...].astype(F32))
    reach = taps.shape[0] - 1
    total = taps[0:1] * ext[8 : 8 + T]
    for lag in range(1, reach + 1):
        total = total + taps[lag : lag + 1] * ext[8 - lag : 8 - lag + T]
    out[...] = (xg[...].astype(F32) * (total + skip[...] * ext[8 : 8 + T])).astype(BF)


def body(Z, U, q, k, v, ck, cv, filled, gain, vb, xg, cstate, cfilter, skip):
    T, D = q.shape
    S = ck.shape[0]
    R = U * T
    H = Z // 2
    taps = jnp.repeat(cfilter, D // cfilter.shape[1], axis=1)
    cstate = jnp.pad(cstate, ((8 - cstate.shape[0], 0), (0, 0)))
    vmem = pl.BlockSpec(memory_space=pltpu.VMEM)
    hbm = pl.BlockSpec(memory_space=pl.ANY)
    dma = pltpu.SemaphoreType.DMA
    return pl.pallas_call(
        functools.partial(kernel, Z, U),
        out_shape=jax.ShapeDtypeStruct((T, D), BF),
        in_specs=[pl.BlockSpec(memory_space=pltpu.SMEM), vmem, vmem, vmem, hbm, hbm] + [vmem] * 6,
        out_specs=vmem,
        scratch_shapes=[
            pltpu.VMEM((Z, 2 * R, DH), BF),
            pltpu.VMEM((2, 2 * R, DH), BF),
            pltpu.VMEM((2, 2, S, DH), BF),
            pltpu.VMEM((S, 2 * DH), BF),
            pltpu.VMEM((S + 2 * R, 2 * DH), BF),
            pltpu.VMEM((DH + FLAG_ROWS, S), BF),
            pltpu.VMEM((DH + FLAG_ROWS, S + 2 * R), BF),
            pltpu.VMEM((Z, 2, DH + FLAG_ROWS, R), F32),
            pltpu.VMEM((Z, 2, 1, R), F32),
            pltpu.VMEM((2, H, 2, DH, R), BF),
            pltpu.VMEM((2, H, 2, DH, R), BF),
            pltpu.VMEM((2, H, 2, 2, R), F32),
            pltpu.VMEM((2, H, 2, 2, R), F32),
            pltpu.VMEM((2 * R, DH), BF),
            pltpu.VMEM((T, D), BF),
            pltpu.VMEM((8, D), BF),
            pltpu.VMEM((8, D), BF),
            pltpu.VMEM((24, D), F32),
            dma((2,)), dma((2,)), dma((2,)),
            dma, dma, dma, dma,
            dma((2, H, 2)), dma((2, H, 2)), dma((2, H, 2)), dma((2, H, 2)), dma((2, H, 2)), dma((2, H, 2)),
            dma, dma, dma, dma,
        ],
        compiler_params=pltpu.CompilerParams(
            collective_id=0, has_side_effects=True, vmem_limit_bytes=52 * 1024 * 1024
        ),
    )(
        filled, q, k, v, ck, cv, gain.reshape(1, D), vb, xg, cstate, taps, skip.reshape(1, D)
    )


def solution(mesh):
    Z, U = mesh.shape["ctx"] // 2, mesh.shape["uly"]
    rows = P(("ctx", "uly"), None)
    return jax.shard_map(
        functools.partial(body, Z, U),
        mesh=mesh,
        in_specs=(rows, rows, rows, P("ctx", "uly"), P("ctx", "uly"), P(), P(), rows, rows, P(), P(), P()),
        out_specs=rows,
        check_vma=False,
    )
```

```python
import functools
import math

import jax
import jax.numpy as jnp
from jax import lax
from jax.experimental import pallas as pl
from jax.experimental.pallas import tpu as pltpu
from jax.sharding import PartitionSpec as P

MESH = pl.DeviceIdType.MESH
DH = 128
FLAG_ROWS = 16
NEG = -1e30
BIG = 1e30
N_AT = 2
BF = jnp.bfloat16
F32 = jnp.float32


def nt(a, b):
    return lax.dot_general(a, b, (((1,), (1,)), ((), ())), preferred_element_type=F32)


def kernel(
    Z, U,
    filled_in, q, k, v, ck, cv, gain_in, vb_in, xg_in, cstate_in, cfilter_in, skip_in,
    out,
    qbuf, kvn, raw, ka, kb, va, vt_b, o_a, m_a, o_s, o_r, s_s, s_r, obuf, att, vb_old, ext,
    gain, vb, xg, cstate, cfilter, skip, taps, filled, s_1, s_2, kvs,
    own_sem, self_sem, x_send, x_recv, q_send, q_recv, n_send, n_recv,
    g_send, g_recv, r_send, r_recv, t_send, t_recv, b_send, b_recv, h_send, h_recv, e_send, e_recv,
):
    T, D = q.shape
    S = ck.shape[0]
    W = 2 * U
    R = U * T
    H = Z // 2
    c_i = lax.axis_index("ctx")
    u = lax.axis_index("uly")
    z, xl = c_i // 2, lax.rem(c_i, 2)
    me = xl * U + u
    head_col = pl.multiple_of((2 * u + xl) * DH, DH)
    scale = math.log2(math.e) / math.sqrt(DH)

    def peer(o):
        return (2 * z + o // U, lax.rem(o, U))

    def ring(d):
        return lax.rem(z + Z + d, Z)

    partner = (2 * z + 1 - xl, u)
    flat = c_i * U + u
    n_dev = 2 * Z * U
    after, before = lax.rem(flat + 1, n_dev), lax.rem(flat + n_dev - 1, n_dev)

    barrier = pltpu.get_barrier_semaphore()

    def greet(i, carry):
        pl.semaphore_signal(barrier, inc=1, device_id=peer(lax.rem(me + i, W)), device_id_type=MESH)
        return carry

    lax.fori_loop(1, W, greet, 0)
    for d in (1, -1, H):
        pl.semaphore_signal(barrier, inc=1, device_id=(2 * ring(d) + xl, u), device_id_type=MESH)
    pl.semaphore_signal(barrier, inc=1, device_id=(before // U, lax.rem(before, U)), device_id_type=MESH)

    @pl.when(me == 0)
    def _():
        def greet_old(i, carry):
            at = (2 * ring(-1) + i // U, lax.rem(i, U))
            pl.semaphore_signal(barrier, inc=1, device_id=at, device_id_type=MESH)
            return carry

        lax.fori_loop(0, W, greet_old, 0)

    my_rows = pl.ds(pl.multiple_of(me * T, T), T)
    mine = pl.multiple_of(xl * DH, DH)
    other = pl.multiple_of((1 - xl) * DH, DH)
    loads = [
        pltpu.make_async_copy(src.at[:, pl.ds(mine, DH)], raw.at[0, i], own_sem.at[i])
        for i, src in enumerate((ck, cv))
    ]
    for load in loads:
        load.start()
    own_cols = pl.ds(head_col, DH)
    selves = [
        pltpu.make_async_copy(q.at[:, own_cols], qbuf.at[z, my_rows], self_sem.at[0]),
        pltpu.make_async_copy(k.at[:, own_cols], kvn.at[0, my_rows], self_sem.at[1]),
        pltpu.make_async_copy(v.at[:, own_cols], kvn.at[1, my_rows], self_sem.at[2]),
    ] + [
        pltpu.make_async_copy(src, dst, self_sem.at[3 + i])
        for i, (src, dst) in enumerate(
            ((gain_in, gain), (vb_in, vb), (xg_in, xg), (cstate_in, cstate), (cfilter_in, cfilter), (skip_in, skip))
        )
    ]
    selves += [pltpu.make_async_copy(src, kvs.at[i], self_sem.at[10 + i]) for i, src in enumerate((k, v))]
    fill = pltpu.make_async_copy(filled_in, filled, self_sem.at[9])
    fill.start()
    for load in selves:
        load.start()
    pl.semaphore_wait(barrier, W + 4)


    def q_copy(o):
        ou, ox = lax.rem(o, U), o // U
        cols = pl.ds(pl.multiple_of((2 * ou + ox) * DH, DH), DH)
        return pltpu.make_async_remote_copy(
            q.at[:, cols], qbuf.at[z, my_rows], q_send, q_recv, device_id=peer(o), device_id_type=MESH
        )

    def n_copy(o):
        ou, ox = lax.rem(o, U), o // U
        cols = pl.ds(pl.multiple_of((2 * ou + ox) * DH, DH), DH)
        return pltpu.make_async_remote_copy(
            kvs.at[:, :, cols], kvn.at[:, my_rows], n_send, n_recv, device_id=peer(o), device_id_type=MESH
        )

    def send_q(i, carry):
        q_copy(lax.rem(me + i, W)).start()
        return carry

    def send_n(i, carry):
        n_copy(lax.rem(me + i, W)).start()
        return carry

    lax.fori_loop(1, W, send_q, 0)
    swaps = [
        pltpu.make_async_remote_copy(
            src.at[:, pl.ds(other, DH)], raw.at[1, i], x_send.at[i], x_recv.at[i],
            device_id=partner, device_id_type=MESH,
        )
        for i, src in enumerate((ck, cv))
    ]
    for swap in swaps:
        swap.start()
    halo = pltpu.make_async_remote_copy(
        vb_in.at[pl.ds(T - 8, 8)], vb_old, h_send, h_recv, device_id=(after // U, lax.rem(after, U)), device_id_type=MESH
    )
    halo.start()

    def split_store(dst, at, x):
        x = x * scale
        hi = x.astype(BF)
        dst[pl.ds(at, x.shape[0]), 0:DH] = hi
        dst[pl.ds(at, x.shape[0]), DH : 2 * DH] = (x - hi.astype(F32)).astype(BF)

    def prepare(which, chunk_ctx, kdst, vdst):
        limit = filled[0] - chunk_ctx * S
        rows = lax.broadcasted_iota(jnp.int32, (S, DH), 0)
        keys = raw[which, 0].astype(F32)
        first = keys[0:1]
        split_store(kdst, 0, jnp.where(rows < limit, keys, first))
        values = jnp.where(rows < limit, raw[which, 1].astype(F32), 0.0)
        vdst[0:DH, 0:S] = values.T.astype(BF)
        lane = lax.broadcasted_iota(jnp.int32, (FLAG_ROWS, S), 1)
        row = lax.broadcasted_iota(jnp.int32, (FLAG_ROWS, S), 0)
        vdst[DH : DH + FLAG_ROWS, 0:S] = jnp.where((row == 0) & (lane < limit), 1.0, 0.0).astype(BF)

    def prepare_new():
        split_store(kb, S, kvn[0].astype(F32))
        vt_b[0:DH, S : S + 2 * R] = kvn[1].astype(F32).T.astype(BF)
        row = lax.broadcasted_iota(jnp.int32, (FLAG_ROWS, 2 * R), 0)
        vt_b[DH : DH + FLAG_ROWS, S : S + 2 * R] = jnp.where(row == 0, 1.0, 0.0).astype(BF)

    fill.wait()
    for load in loads:
        load.wait()
    prepare(0, c_i, ka, va)
    for load in selves:
        load.wait()

    n_taps, n_groups = cfilter.shape
    f_1 = cfilter[...]
    f_hi = f_1.astype(BF)
    f_2 = f_1 - f_hi.astype(F32)
    f_mid = f_2.astype(BF)
    f_lo = (f_2 - f_mid.astype(F32)).astype(BF)
    wide = min(512, D)

    def spread(i, carry):
        cols = pl.ds(pl.multiple_of(i * wide, wide), wide)
        group = lax.broadcasted_iota(jnp.int32, (n_groups, wide), 0) * (D // n_groups)
        off = i * wide + lax.broadcasted_iota(jnp.int32, (n_groups, wide), 1) - group
        pick = jnp.where((off >= 0) & (off < D // n_groups), 1.0, 0.0).astype(BF)
        one = functools.partial(jnp.dot, preferred_element_type=F32)
        taps[:, cols] = one(f_hi, pick) + one(f_mid, pick) + one(f_lo, pick)
        return carry

    lax.fori_loop(0, D // wide, spread, 0)

    def twice(zq, half):
        x = qbuf[zq, pl.ds(pl.multiple_of(half * R, R), R), :]
        return jnp.concatenate([x, x], axis=1)

    def has_slots(chunk_ctx):
        return jnp.broadcast_to(filled[0] - chunk_ctx * S, (1, R)) > 0

    def first_scores(slot, zq, half):
        s_1[slot] = nt(ka[...], twice(zq, half))

    def first_part(slot, zq, half):
        s = s_1[slot]
        top = jnp.max(s, axis=0, keepdims=True)
        p = jnp.exp2(s - top).astype(BF)
        o_a[zq, half] = jnp.dot(va[...], p, preferred_element_type=F32)
        m_a[zq, half] = jnp.where(has_slots(c_i), top, NEG)

    def q_hop(way, dist, half, zq):
        rows = pl.ds(pl.multiple_of(half * R, R), R)
        return pltpu.make_async_remote_copy(
            qbuf.at[zq, rows], qbuf.at[zq, rows], g_send.at[way, dist, half], g_recv.at[way, dist, half],
            device_id=(2 * ring(jnp.where(dist == H - 1, H, 1 - 2 * way)) + xl, u), device_id_type=MESH,
        )

    everyone = pl.ds(0, (W - 1) * T)
    pltpu.make_async_copy(qbuf.at[z, everyone], qbuf.at[z, everyone], q_recv).wait()
    for way in (0, 1):
        q_hop(way, H - 1, way, z).start()
    if H > 1:
        for i in (0, 1):
            for way in (0, 1):
                q_hop(way, 0, (way + i) % 2, z).start()

    steps = 2 * Z

    def arrival(t):
        early, far, late = t < 2, (t >= steps - 6) & (t < steps - 4), t >= steps - 4
        j = jnp.where(late, t - (steps - 4), lax.rem(t + 2, 4))
        way = jnp.where(early, 0, jnp.where(far, t - (steps - 6), lax.rem(j, 2)))
        half = jnp.where(early, t, jnp.where(far, t - (steps - 6), jnp.where(j < 2, lax.rem(j, 2), 1 - lax.rem(j, 2))))
        dist = jnp.where(early, 0, jnp.where(far, H, jnp.where(late, H - 1, (t + 2) // 4)))
        return way, half, dist, ring(dist * (2 * way - 1))

    def second_scores(slot, zq, half):
        s_2[slot] = nt(kb[...], twice(zq, half))

    def second_part(slot, zq, half):
        s = s_2[slot]
        s_c, s_n = s[0:S], s[S : S + 2 * R]
        key_at = z * (2 * R) + lax.broadcasted_iota(jnp.int32, (2 * R, R), 0)
        token_at = zq * (2 * R) + half * R + lax.broadcasted_iota(jnp.int32, (2 * R, R), 1)
        s_n = jnp.where(key_at <= token_at, s_n, NEG)
        filled_here = has_slots(2 * z + 1 - xl)
        top_c = jnp.where(filled_here, jnp.max(s_c, axis=0, keepdims=True), NEG)
        m_1 = m_a[zq, half]
        top = jnp.maximum(jnp.maximum(top_c, m_1), jnp.max(s_n, axis=0, keepdims=True))
        p_c = jnp.exp2(s_c - jnp.where(filled_here, top, BIG)).astype(BF)
        p_n = jnp.exp2(s_n - top).astype(BF)
        o = o_a[zq, half] * jnp.exp2(m_1 - top)
        o = o + jnp.dot(vt_b[...], jnp.concatenate([p_c, p_n], axis=0), preferred_element_type=F32)
        o_a[zq, half] = o
        m_a[zq, half] = top

    def arrive(t, slot):
        way, half, dist, zq = arrival(t)

        @pl.when(t >= 2)
        def _():
            q_hop(way, dist - 1, half, zq).wait_recv()

            @pl.when(dist < H - 1)
            def _():
                q_hop(way, dist, half, zq).start()

        first_scores(slot, zq, half)

    def weigh(t, slot):
        _, half, _, zq = arrival(t)
        first_part(slot, zq, half)

    def gather(begin, end):
        def pair(i, carry):
            t = begin + 2 * i
            arrive(t + 1, 1)
            weigh(t, 0)

            if begin == 0:
                @pl.when(i == min(N_AT, (end - begin) // 2 - 2))
                def _():
                    lax.fori_loop(1, W, send_n, 0)

            arrive(t + 2, 0)
            weigh(t + 1, 1)
            return carry

        arrive(jnp.int32(begin), 0)
        lax.fori_loop(0, (end - begin) // 2 - 1, pair, 0)
        arrive(jnp.int32(end - 1), 1)
        weigh(jnp.int32(end - 2), 0)
        weigh(jnp.int32(end - 1), 1)

    gather(0, steps - 4)
    pltpu.make_async_copy(kvn.at[:, everyone], kvn.at[:, everyone], n_recv).wait()
    prepare_new()
    for swap in swaps:
        swap.wait_recv()
    prepare(1, 2 * z + 1 - xl, kb, vt_b)

    def o_hop(way, slot, half):
        to = (2 * ring(1 - 2 * way) + xl, u)
        return (
            pltpu.make_async_remote_copy(
                o_s.at[way, slot, half], o_r.at[way, slot, half], r_send.at[way, slot, half],
                r_recv.at[way, slot, half], device_id=to, device_id_type=MESH,
            ),
            pltpu.make_async_remote_copy(
                s_s.at[way, slot, half], s_r.at[way, slot, half], t_send.at[way, slot, half],
                t_recv.at[way, slot, half], device_id=to, device_id_type=MESH,
            ),
        )

    def merge(zq, half, way, slot):
        for hop in o_hop(way, slot, half):
            hop.wait_recv()
        m_1 = m_a[zq, half]
        m_2 = s_r[way, slot, half, 0:1]
        top = jnp.maximum(m_1, m_2)
        f_1, f_2 = jnp.exp2(m_1 - top), jnp.exp2(m_2 - top)
        m_a[zq, half] = top
        o_a[zq, half, 0:DH] = o_a[zq, half, 0:DH] * f_1 + o_r[way, slot, half].astype(F32) * f_2
        o_a[zq, half, DH : DH + 1] = o_a[zq, half, DH : DH + 1] * f_1 + s_r[way, slot, half, 1:2] * f_2

    def back(o):
        return pltpu.make_async_remote_copy(
            obuf.at[pl.ds(2 * o, 3)], att.at[:, :, own_cols], b_send, b_recv, device_id=peer(o), device_id_type=MESH
        )

    def back_first():
        return pltpu.make_async_remote_copy(
            obuf.at[pl.ds(1, 2)], att.at[pl.ds(1, 2), :, own_cols], b_send, b_recv, device_id=peer(0), device_id_type=MESH
        )

    edge = pltpu.make_async_remote_copy(
        obuf.at[pl.ds(2 * W, 1)], att.at[pl.ds(0, 1), :, own_cols], e_send, e_recv,
        device_id=(2 * ring(1), 0), device_id_type=MESH,
    )

    def departure(t):
        first, own = t < 2, t >= steps - 2
        j = lax.rem(t + 2, 4)
        half = jnp.where(first, t, jnp.where(own, t - (steps - 2), lax.rem(j, 2)))
        way = jnp.where(first, t, jnp.where(j < 2, 1 - lax.rem(j, 2), lax.rem(j, 2)))
        dist = jnp.where(first, H, jnp.where(own, 0, H - (t + 2) // 4))
        return way, half, dist, ring(dist * (1 - 2 * way))

    def score(t, slot):
        _, half, _, zq = departure(t)
        second_scores(slot, zq, half)

    def ship(t, slot):
        way, half, dist, zq = departure(t)
        own = t >= steps - 2
        second_part(slot, zq, half)

        @pl.when(jnp.logical_not(own))
        def _():
            @pl.when((dist < H - 1) | ((dist == H - 1) & (half == way)))
            def _():
                merge(zq, half, way, dist)

            slot = dist - 1
            o_s[way, slot, half] = o_a[zq, half, 0:DH].astype(BF)
            s_s[way, slot, half, 0:1] = m_a[zq, half]
            s_s[way, slot, half, 1:2] = o_a[zq, half, DH : DH + 1]
            for hop in o_hop(way, slot, half):
                hop.start()

        @pl.when(own)
        def _():
            merge(z, half, 0, 0)
            merge(z, half, 1, 0)
            done = o_a[z, half, 0:DH] / o_a[z, half, DH : DH + 1]
            obuf[pl.ds(1 + half * (R // 8), R // 8)] = done.T.reshape(R // 8, 8, DH).astype(BF)

            def send_back(i, c):
                o = half * U + lax.rem(u + i, U)

                @pl.when((o != me) & (o > 0))
                def _():
                    back(o).start()

                @pl.when((o != me) & (o == 0))
                def _():
                    back_first().start()

                return c

            lax.fori_loop(0, U, send_back, 0)

    def scatter_pair(i, carry):
        score(2 * i + 1, 1)
        ship(2 * i, 0)
        score(jnp.minimum(2 * i + 2, steps - 1), 0)
        ship(2 * i + 1, 1)
        return carry

    for t in (0, 1):
        score(jnp.int32(t), t)
    for t in (0, 1):
        ship(jnp.int32(t), t)
    gather(steps - 4, steps)
    score(jnp.int32(2), 0)
    lax.fori_loop(1, steps // 2, scatter_pair, 0)
    edge.start()

    @pl.when(me == 0)
    def _():
        att[1:3, :, own_cols] = obuf[1:3]

    @pl.when(me > 0)
    def _():
        att[:, :, own_cols] = obuf[pl.ds(2 * me, 3)]

    pltpu.make_async_copy(qbuf.at[z, everyone], qbuf.at[z, everyone], q_send).wait()
    pltpu.make_async_copy(kvn.at[:, everyone], kvn.at[:, everyone], n_send).wait()
    for swap in swaps:
        swap.wait_send()
    halo.wait()
    for way in (0, 1):
        for half in (0, 1):
            for d in range(H):
                if d < H - 1 or half == way:
                    q_hop(way, d, half, z).wait_send()
                    for hop in o_hop(way, d, half):
                        hop.wait_send()

    def bytes_of(blocks, columns, sem):
        part = att.at[pl.ds(0, blocks), :, pl.ds(0, columns)]
        return pltpu.make_async_copy(part, part, sem)

    @pl.when(me == 0)
    def _():
        bytes_of(2, (W - 1) * DH, b_recv).wait()
        bytes_of(3, (W - 1) * DH, b_send).wait()
        bytes_of(1, W * DH, e_recv).wait()

    @pl.when(me > 0)
    def _():
        bytes_of(3, (W - 1) * DH, b_recv).wait()
        bytes_of(3, (W - 2) * DH, b_send).wait()
        bytes_of(2, DH, b_send).wait()

    edge.wait_send()

    for i in range(3):
        x = att[i].astype(F32)
        inv = lax.rsqrt(jnp.mean(x * x, axis=1, keepdims=True) + 1e-06)
        branch = vb_old[...] if i == 0 else vb[8 * (i - 1) : 8 * i]
        ext[8 * i : 8 * i + 8, :] = (x * inv * gain[...] * branch.astype(F32)).astype(BF).astype(F32)

    @pl.when(flat == 0)
    def _():
        ext[8 - cstate.shape[0] : 8, :] = cstate[...].astype(F32)

    total = taps[0:1] * ext[8 : 8 + T]
    for lag in range(1, n_taps):
        total = total + taps[lag : lag + 1] * ext[8 - lag : 8 - lag + T]
    out[...] = (xg[...].astype(F32) * (total + skip[...] * ext[8 : 8 + T])).astype(BF)


def body(Z, U, q, k, v, ck, cv, filled, gain, vb, xg, cstate, cfilter, skip):
    T, D = q.shape
    S = ck.shape[0]
    R = U * T
    H = Z // 2
    vmem = pl.BlockSpec(memory_space=pltpu.VMEM)
    hbm = pl.BlockSpec(memory_space=pltpu.HBM)
    dma = pltpu.SemaphoreType.DMA
    return pl.pallas_call(
        functools.partial(kernel, Z, U),
        out_shape=jax.ShapeDtypeStruct((T, D), BF),
        in_specs=[hbm] * 12,
        out_specs=vmem,
        scratch_shapes=[
            pltpu.VMEM((Z, 2 * R, DH), BF),
            pltpu.VMEM((2, 2 * R, DH), BF),
            pltpu.VMEM((2, 2, S, DH), BF),
            pltpu.VMEM((S, 2 * DH), BF),
            pltpu.VMEM((S + 2 * R, 2 * DH), BF),
            pltpu.VMEM((DH + FLAG_ROWS, S), BF),
            pltpu.VMEM((DH + FLAG_ROWS, S + 2 * R), BF),
            pltpu.VMEM((Z, 2, DH + FLAG_ROWS, R), F32),
            pltpu.VMEM((Z, 2, 1, R), F32),
            pltpu.VMEM((2, H, 2, DH, R), BF),
            pltpu.VMEM((2, H, 2, DH, R), BF),
            pltpu.VMEM((2, H, 2, 2, R), F32),
            pltpu.VMEM((2, H, 2, 2, R), F32),
            pltpu.VMEM((1 + 2 * R // 8, 8, DH), BF),
            pltpu.VMEM((3, 8, D), BF),
            pltpu.VMEM((8, D), BF),
            pltpu.VMEM((24, D), F32),
            pltpu.VMEM((1, D), F32),
            pltpu.VMEM((T, D), BF),
            pltpu.VMEM((T, D), BF),
            pltpu.VMEM(cstate.shape, BF),
            pltpu.VMEM(cfilter.shape, F32),
            pltpu.VMEM((1, D), F32),
            pltpu.VMEM((cfilter.shape[0], D), F32),
            pltpu.SMEM((1,), jnp.int32),
            pltpu.VMEM((2, S, R), F32),
            pltpu.VMEM((2, S + 2 * R, R), F32),
            pltpu.VMEM((2, T, D), BF),
            dma((2,)), dma((12,)), dma((2,)), dma((2,)),
            dma, dma, dma, dma,
            dma((2, H, 2)), dma((2, H, 2)), dma((2, H, 2)), dma((2, H, 2)), dma((2, H, 2)), dma((2, H, 2)),
            dma, dma, dma, dma, dma, dma,
        ],
        compiler_params=pltpu.CompilerParams(
            collective_id=0, has_side_effects=True, vmem_limit_bytes=61 * 1024 * 1024
        ),
    )(
        filled, q, k, v, ck, cv, gain.reshape(1, D), vb, xg, cstate, cfilter, skip.reshape(1, D)
    )


def solution(mesh):
    Z, U = mesh.shape["ctx"] // 2, mesh.shape["uly"]
    rows = P(("ctx", "uly"), None)
    return jax.shard_map(
        functools.partial(body, Z, U),
        mesh=mesh,
        in_specs=(rows, rows, rows, P("ctx", "uly"), P("ctx", "uly"), P(), P(), rows, rows, P(), P(), P()),
        out_specs=rows,
        check_vma=False,
    )
```

```python
import functools
import math

import jax
import jax.numpy as jnp
from jax import lax
from jax.experimental import pallas as pl
from jax.experimental.pallas import tpu as pltpu
from jax.sharding import PartitionSpec as P

MESH = pl.DeviceIdType.MESH
DH = 128
FLAG_ROWS = 16
NEG = -1e30
BIG = 1e30
N_AT = 2
BF = jnp.bfloat16
F32 = jnp.float32


def nt(a, b):
    return lax.dot_general(a, b, (((1,), (1,)), ((), ())), preferred_element_type=F32)


def kernel(
    Z, U,
    filled_in, q, k, v, ck, cv, gain_in, vb_in, xg_in, cstate_in, cfilter_in, skip_in,
    out,
    qbuf, kvn, raw, ka, kb, va, vt_b, o_a, m_a, o_s, o_r, s_s, s_r, obuf, att, vb_old, ext,
    gain, vb, xg, cstate, cfilter, skip, taps, filled, s_1, s_2, kvs,
    own_sem, self_sem, x_send, x_recv, q_send, q_recv, n_send, n_recv,
    g_send, g_recv, r_send, r_recv, t_send, t_recv, b_send, b_recv, h_send, h_recv, e_send, e_recv,
):
    T, D = q.shape
    S = ck.shape[0]
    W = 2 * U
    R = U * T
    H = Z // 2
    c_i = lax.axis_index("ctx")
    u = lax.axis_index("uly")
    z, xl = c_i // 2, lax.rem(c_i, 2)
    me = xl * U + u
    head_col = pl.multiple_of((2 * u + xl) * DH, DH)
    scale = math.log2(math.e) / math.sqrt(DH)

    def peer(o):
        return (2 * z + o // U, lax.rem(o, U))

    def ring(d):
        return lax.rem(z + Z + d, Z)

    partner = (2 * z + 1 - xl, u)
    flat = c_i * U + u
    n_dev = 2 * Z * U
    after, before = lax.rem(flat + 1, n_dev), lax.rem(flat + n_dev - 1, n_dev)

    barrier = pltpu.get_barrier_semaphore()

    def greet(i, carry):
        pl.semaphore_signal(barrier, inc=1, device_id=peer(lax.rem(me + i, W)), device_id_type=MESH)
        return carry

    lax.fori_loop(1, W, greet, 0)
    for d in (1, -1):
        pl.semaphore_signal(barrier, inc=1, device_id=(2 * ring(d) + xl, u), device_id_type=MESH)
    pl.semaphore_signal(barrier, inc=1, device_id=(before // U, lax.rem(before, U)), device_id_type=MESH)

    @pl.when(me == 0)
    def _():
        def greet_old(i, carry):
            at = (2 * ring(-1) + i // U, lax.rem(i, U))
            pl.semaphore_signal(barrier, inc=1, device_id=at, device_id_type=MESH)
            return carry

        lax.fori_loop(0, W, greet_old, 0)

    my_rows = pl.ds(pl.multiple_of(me * T, T), T)
    mine = pl.multiple_of(xl * DH, DH)
    other = pl.multiple_of((1 - xl) * DH, DH)
    loads = [
        pltpu.make_async_copy(src.at[:, pl.ds(mine, DH)], raw.at[0, i], own_sem.at[i])
        for i, src in enumerate((ck, cv))
    ]
    for load in loads:
        load.start()
    own_cols = pl.ds(head_col, DH)
    selves = [
        pltpu.make_async_copy(q.at[:, own_cols], qbuf.at[z, my_rows], self_sem.at[0]),
        pltpu.make_async_copy(k.at[:, own_cols], kvn.at[0, my_rows], self_sem.at[1]),
        pltpu.make_async_copy(v.at[:, own_cols], kvn.at[1, my_rows], self_sem.at[2]),
    ] + [
        pltpu.make_async_copy(src, dst, self_sem.at[3 + i])
        for i, (src, dst) in enumerate(
            ((gain_in, gain), (vb_in, vb), (xg_in, xg), (cstate_in, cstate), (cfilter_in, cfilter), (skip_in, skip))
        )
    ]
    selves += [pltpu.make_async_copy(src, kvs.at[i], self_sem.at[10 + i]) for i, src in enumerate((k, v))]
    fill = pltpu.make_async_copy(filled_in, filled, self_sem.at[9])
    fill.start()
    for load in selves:
        load.start()
    pl.semaphore_wait(barrier, W + 3)


    def q_copy(o):
        ou, ox = lax.rem(o, U), o // U
        cols = pl.ds(pl.multiple_of((2 * ou + ox) * DH, DH), DH)
        return pltpu.make_async_remote_copy(
            q.at[:, cols], qbuf.at[z, my_rows], q_send, q_recv, device_id=peer(o), device_id_type=MESH
        )

    def n_copy(o):
        ou, ox = lax.rem(o, U), o // U
        cols = pl.ds(pl.multiple_of((2 * ou + ox) * DH, DH), DH)
        return pltpu.make_async_remote_copy(
            kvs.at[:, :, cols], kvn.at[:, my_rows], n_send, n_recv, device_id=peer(o), device_id_type=MESH
        )

    def send_q(i, carry):
        q_copy(lax.rem(me + i, W)).start()
        return carry

    def send_n(i, carry):
        n_copy(lax.rem(me + i, W)).start()
        return carry

    lax.fori_loop(1, W, send_q, 0)
    swaps = [
        pltpu.make_async_remote_copy(
            src.at[:, pl.ds(other, DH)], raw.at[1, i], x_send.at[i], x_recv.at[i],
            device_id=partner, device_id_type=MESH,
        )
        for i, src in enumerate((ck, cv))
    ]
    for swap in swaps:
        swap.start()
    halo = pltpu.make_async_remote_copy(
        vb_in.at[pl.ds(T - 8, 8)], vb_old, h_send, h_recv, device_id=(after // U, lax.rem(after, U)), device_id_type=MESH
    )
    halo.start()

    def split_store(dst, at, x):
        x = x * scale
        hi = x.astype(BF)
        dst[pl.ds(at, x.shape[0]), 0:DH] = hi
        dst[pl.ds(at, x.shape[0]), DH : 2 * DH] = (x - hi.astype(F32)).astype(BF)

    def prepare(which, chunk_ctx, kdst, vdst):
        limit = filled[0] - chunk_ctx * S
        rows = lax.broadcasted_iota(jnp.int32, (S, DH), 0)
        keys = raw[which, 0].astype(F32)
        first = keys[0:1]
        split_store(kdst, 0, jnp.where(rows < limit, keys, first))
        values = jnp.where(rows < limit, raw[which, 1].astype(F32), 0.0)
        vdst[0:DH, 0:S] = values.T.astype(BF)
        lane = lax.broadcasted_iota(jnp.int32, (FLAG_ROWS, S), 1)
        row = lax.broadcasted_iota(jnp.int32, (FLAG_ROWS, S), 0)
        vdst[DH : DH + FLAG_ROWS, 0:S] = jnp.where((row == 0) & (lane < limit), 1.0, 0.0).astype(BF)

    def prepare_new():
        split_store(kb, S, kvn[0].astype(F32))
        vt_b[0:DH, S : S + 2 * R] = kvn[1].astype(F32).T.astype(BF)
        row = lax.broadcasted_iota(jnp.int32, (FLAG_ROWS, 2 * R), 0)
        vt_b[DH : DH + FLAG_ROWS, S : S + 2 * R] = jnp.where(row == 0, 1.0, 0.0).astype(BF)

    fill.wait()
    for load in loads:
        load.wait()
    prepare(0, c_i, ka, va)
    for load in selves:
        load.wait()

    n_taps, n_groups = cfilter.shape
    f_1 = cfilter[...]
    f_hi = f_1.astype(BF)
    f_2 = f_1 - f_hi.astype(F32)
    f_mid = f_2.astype(BF)
    f_lo = (f_2 - f_mid.astype(F32)).astype(BF)
    wide = min(512, D)

    def spread(i, carry):
        cols = pl.ds(pl.multiple_of(i * wide, wide), wide)
        group = lax.broadcasted_iota(jnp.int32, (n_groups, wide), 0) * (D // n_groups)
        off = i * wide + lax.broadcasted_iota(jnp.int32, (n_groups, wide), 1) - group
        pick = jnp.where((off >= 0) & (off < D // n_groups), 1.0, 0.0).astype(BF)
        one = functools.partial(jnp.dot, preferred_element_type=F32)
        taps[:, cols] = one(f_hi, pick) + one(f_mid, pick) + one(f_lo, pick)
        return carry

    lax.fori_loop(0, D // wide, spread, 0)

    def twice(zq, half):
        x = qbuf[zq, pl.ds(pl.multiple_of(half * R, R), R), :]
        return jnp.concatenate([x, x], axis=1)

    def has_slots(chunk_ctx):
        return jnp.broadcast_to(filled[0] - chunk_ctx * S, (1, R)) > 0

    def first_scores(slot, zq, half):
        s_1[slot] = nt(ka[...], twice(zq, half))

    def first_part(slot, zq, half):
        s = s_1[slot]
        top = jnp.max(s, axis=0, keepdims=True)
        p = jnp.exp2(s - top).astype(BF)
        o_a[zq, half] = jnp.dot(va[...], p, preferred_element_type=F32)
        m_a[zq, half] = jnp.where(has_slots(c_i), top, NEG)

    def q_hop(way, dist, half, zq):
        rows = pl.ds(pl.multiple_of(half * R, R), R)
        return pltpu.make_async_remote_copy(
            qbuf.at[zq, rows], qbuf.at[zq, rows], g_send.at[way, dist, half], g_recv.at[way, dist, half],
            device_id=(2 * ring(1 - 2 * way) + xl, u), device_id_type=MESH,
        )

    everyone = pl.ds(0, (W - 1) * T)
    pltpu.make_async_copy(qbuf.at[z, everyone], qbuf.at[z, everyone], q_recv).wait()
    if H > 1:
        for i in (0, 1):
            for way in (0, 1):
                q_hop(way, 0, (way + i) % 2, z).start()

    steps = 2 * Z

    def arrival(t):
        early, far = t < 2, t >= steps - 2
        j = lax.rem(t + 2, 4)
        way = jnp.where(early, 0, jnp.where(far, t - (steps - 2), lax.rem(j, 2)))
        half = jnp.where(early, t, jnp.where(far, t - (steps - 2), jnp.where(j < 2, lax.rem(j, 2), 1 - lax.rem(j, 2))))
        dist = jnp.where(early, 0, jnp.where(far, H, (t + 2) // 4))
        return way, half, dist, ring(dist * (2 * way - 1))

    def second_scores(slot, zq, half):
        s_2[slot] = nt(kb[...], twice(zq, half))

    def second_part(slot, zq, half):
        s = s_2[slot]
        s_c, s_n = s[0:S], s[S : S + 2 * R]
        key_at = z * (2 * R) + lax.broadcasted_iota(jnp.int32, (2 * R, R), 0)
        token_at = zq * (2 * R) + half * R + lax.broadcasted_iota(jnp.int32, (2 * R, R), 1)
        s_n = jnp.where(key_at <= token_at, s_n, NEG)
        filled_here = has_slots(2 * z + 1 - xl)
        top_c = jnp.where(filled_here, jnp.max(s_c, axis=0, keepdims=True), NEG)
        m_1 = m_a[zq, half]
        top = jnp.maximum(jnp.maximum(top_c, m_1), jnp.max(s_n, axis=0, keepdims=True))
        p_c = jnp.exp2(s_c - jnp.where(filled_here, top, BIG)).astype(BF)
        p_n = jnp.exp2(s_n - top).astype(BF)
        o = o_a[zq, half] * jnp.exp2(m_1 - top)
        o = o + jnp.dot(vt_b[...], jnp.concatenate([p_c, p_n], axis=0), preferred_element_type=F32)
        o_a[zq, half] = o
        m_a[zq, half] = top

    def arrive(t, slot):
        way, half, dist, zq = arrival(t)

        @pl.when(t >= 2)
        def _():
            q_hop(way, dist - 1, half, zq).wait_recv()

            @pl.when((dist < H - 1) | ((dist == H - 1) & (half == way)))
            def _():
                q_hop(way, dist, half, zq).start()

        first_scores(slot, zq, half)

    def weigh(t, slot):
        _, half, _, zq = arrival(t)
        first_part(slot, zq, half)

    def gather(begin, end):
        def pair(i, carry):
            t = begin + 2 * i
            arrive(t + 1, 1)
            weigh(t, 0)

            if begin == 0:
                @pl.when(i == min(N_AT, (end - begin) // 2 - 2))
                def _():
                    lax.fori_loop(1, W, send_n, 0)

            arrive(t + 2, 0)
            weigh(t + 1, 1)
            return carry

        arrive(jnp.int32(begin), 0)
        lax.fori_loop(0, (end - begin) // 2 - 1, pair, 0)
        arrive(jnp.int32(end - 1), 1)
        weigh(jnp.int32(end - 2), 0)
        weigh(jnp.int32(end - 1), 1)

    gather(0, steps - 2)
    for swap in swaps:
        swap.wait_recv()
    prepare(1, 2 * z + 1 - xl, kb, vt_b)
    pltpu.make_async_copy(kvn.at[:, everyone], kvn.at[:, everyone], n_recv).wait()
    prepare_new()

    def o_hop(way, slot, half):
        to = (2 * ring(1 - 2 * way) + xl, u)
        return (
            pltpu.make_async_remote_copy(
                o_s.at[way, slot, half], o_r.at[way, slot, half], r_send.at[way, slot, half],
                r_recv.at[way, slot, half], device_id=to, device_id_type=MESH,
            ),
            pltpu.make_async_remote_copy(
                s_s.at[way, slot, half], s_r.at[way, slot, half], t_send.at[way, slot, half],
                t_recv.at[way, slot, half], device_id=to, device_id_type=MESH,
            ),
        )

    def merge(zq, half, way, slot):
        for hop in o_hop(way, slot, half):
            hop.wait_recv()
        m_1 = m_a[zq, half]
        m_2 = s_r[way, slot, half, 0:1]
        top = jnp.maximum(m_1, m_2)
        f_1, f_2 = jnp.exp2(m_1 - top), jnp.exp2(m_2 - top)
        m_a[zq, half] = top
        o_a[zq, half, 0:DH] = o_a[zq, half, 0:DH] * f_1 + o_r[way, slot, half].astype(F32) * f_2
        o_a[zq, half, DH : DH + 1] = o_a[zq, half, DH : DH + 1] * f_1 + s_r[way, slot, half, 1:2] * f_2

    def back(o):
        return pltpu.make_async_remote_copy(
            obuf.at[pl.ds(2 * o, 3)], att.at[:, :, own_cols], b_send, b_recv, device_id=peer(o), device_id_type=MESH
        )

    def back_first():
        return pltpu.make_async_remote_copy(
            obuf.at[pl.ds(1, 2)], att.at[pl.ds(1, 2), :, own_cols], b_send, b_recv, device_id=peer(0), device_id_type=MESH
        )

    edge = pltpu.make_async_remote_copy(
        obuf.at[pl.ds(2 * W, 1)], att.at[pl.ds(0, 1), :, own_cols], e_send, e_recv,
        device_id=(2 * ring(1), 0), device_id_type=MESH,
    )

    def departure(t):
        first, own = t < 2, t >= steps - 2
        j = lax.rem(t + 2, 4)
        half = jnp.where(first, t, jnp.where(own, t - (steps - 2), lax.rem(j, 2)))
        way = jnp.where(first, t, jnp.where(j < 2, 1 - lax.rem(j, 2), lax.rem(j, 2)))
        dist = jnp.where(first, H, jnp.where(own, 0, H - (t + 2) // 4))
        return way, half, dist, ring(dist * (1 - 2 * way))

    def score(t, slot):
        _, half, _, zq = departure(t)
        second_scores(slot, zq, half)

    def ship(t, slot):
        way, half, dist, zq = departure(t)
        own = t >= steps - 2
        second_part(slot, zq, half)

        @pl.when(jnp.logical_not(own))
        def _():
            @pl.when((dist < H - 1) | ((dist == H - 1) & (half == way)))
            def _():
                merge(zq, half, way, dist)

            slot = dist - 1
            o_s[way, slot, half] = o_a[zq, half, 0:DH].astype(BF)
            s_s[way, slot, half, 0:1] = m_a[zq, half]
            s_s[way, slot, half, 1:2] = o_a[zq, half, DH : DH + 1]
            for hop in o_hop(way, slot, half):
                hop.start()

        @pl.when(own)
        def _():
            merge(z, half, 0, 0)
            merge(z, half, 1, 0)
            done = o_a[z, half, 0:DH] / o_a[z, half, DH : DH + 1]
            obuf[pl.ds(1 + half * (R // 8), R // 8)] = done.T.reshape(R // 8, 8, DH).astype(BF)

            def send_back(i, c):
                o = half * U + lax.rem(u + i, U)

                @pl.when((o != me) & (o > 0))
                def _():
                    back(o).start()

                @pl.when((o != me) & (o == 0))
                def _():
                    back_first().start()

                return c

            lax.fori_loop(0, U, send_back, 0)

    def scatter_pair(i, carry):
        score(2 * i + 1, 1)
        ship(2 * i, 0)
        score(jnp.minimum(2 * i + 2, steps - 1), 0)
        ship(2 * i + 1, 1)
        return carry

    for t in (0, 1):
        arrive(jnp.int32(steps - 2 + t), t)
        if t == 1:
            ship(jnp.int32(0), 0)
        score(jnp.int32(t), t)
        weigh(jnp.int32(steps - 2 + t), t)
    ship(jnp.int32(1), 1)
    score(jnp.int32(2), 0)
    lax.fori_loop(1, steps // 2, scatter_pair, 0)
    edge.start()

    @pl.when(me == 0)
    def _():
        att[1:3, :, own_cols] = obuf[1:3]

    @pl.when(me > 0)
    def _():
        att[:, :, own_cols] = obuf[pl.ds(2 * me, 3)]

    pltpu.make_async_copy(qbuf.at[z, everyone], qbuf.at[z, everyone], q_send).wait()
    pltpu.make_async_copy(kvn.at[:, everyone], kvn.at[:, everyone], n_send).wait()
    for swap in swaps:
        swap.wait_send()
    halo.wait()
    for way in (0, 1):
        for half in (0, 1):
            for d in range(H):
                if d < H - 1 or half == way:
                    q_hop(way, d, half, z).wait_send()
                    for hop in o_hop(way, d, half):
                        hop.wait_send()

    def bytes_of(blocks, columns, sem):
        part = att.at[pl.ds(0, blocks), :, pl.ds(0, columns)]
        return pltpu.make_async_copy(part, part, sem)

    @pl.when(me == 0)
    def _():
        bytes_of(2, (W - 1) * DH, b_recv).wait()
        bytes_of(3, (W - 1) * DH, b_send).wait()
        bytes_of(1, W * DH, e_recv).wait()

    @pl.when(me > 0)
    def _():
        bytes_of(3, (W - 1) * DH, b_recv).wait()
        bytes_of(3, (W - 2) * DH, b_send).wait()
        bytes_of(2, DH, b_send).wait()

    edge.wait_send()

    for i in range(3):
        x = att[i].astype(F32)
        inv = lax.rsqrt(jnp.mean(x * x, axis=1, keepdims=True) + 1e-06)
        branch = vb_old[...] if i == 0 else vb[8 * (i - 1) : 8 * i]
        ext[8 * i : 8 * i + 8, :] = (x * inv * gain[...] * branch.astype(F32)).astype(BF).astype(F32)

    @pl.when(flat == 0)
    def _():
        ext[8 - cstate.shape[0] : 8, :] = cstate[...].astype(F32)

    total = taps[0:1] * ext[8 : 8 + T]
    for lag in range(1, n_taps):
        total = total + taps[lag : lag + 1] * ext[8 - lag : 8 - lag + T]
    out[...] = (xg[...].astype(F32) * (total + skip[...] * ext[8 : 8 + T])).astype(BF)


def body(Z, U, q, k, v, ck, cv, filled, gain, vb, xg, cstate, cfilter, skip):
    T, D = q.shape
    S = ck.shape[0]
    R = U * T
    H = Z // 2
    vmem = pl.BlockSpec(memory_space=pltpu.VMEM)
    hbm = pl.BlockSpec(memory_space=pltpu.HBM)
    dma = pltpu.SemaphoreType.DMA
    return pl.pallas_call(
        functools.partial(kernel, Z, U),
        out_shape=jax.ShapeDtypeStruct((T, D), BF),
        in_specs=[hbm] * 12,
        out_specs=vmem,
        scratch_shapes=[
            pltpu.VMEM((Z, 2 * R, DH), BF),
            pltpu.VMEM((2, 2 * R, DH), BF),
            pltpu.VMEM((2, 2, S, DH), BF),
            pltpu.VMEM((S, 2 * DH), BF),
            pltpu.VMEM((S + 2 * R, 2 * DH), BF),
            pltpu.VMEM((DH + FLAG_ROWS, S), BF),
            pltpu.VMEM((DH + FLAG_ROWS, S + 2 * R), BF),
            pltpu.VMEM((Z, 2, DH + FLAG_ROWS, R), F32),
            pltpu.VMEM((Z, 2, 1, R), F32),
            pltpu.VMEM((2, H, 2, DH, R), BF),
            pltpu.VMEM((2, H, 2, DH, R), BF),
            pltpu.VMEM((2, H, 2, 2, R), F32),
            pltpu.VMEM((2, H, 2, 2, R), F32),
            pltpu.VMEM((1 + 2 * R // 8, 8, DH), BF),
            pltpu.VMEM((3, 8, D), BF),
            pltpu.VMEM((8, D), BF),
            pltpu.VMEM((24, D), F32),
            pltpu.VMEM((1, D), F32),
            pltpu.VMEM((T, D), BF),
            pltpu.VMEM((T, D), BF),
            pltpu.VMEM(cstate.shape, BF),
            pltpu.VMEM(cfilter.shape, F32),
            pltpu.VMEM((1, D), F32),
            pltpu.VMEM((cfilter.shape[0], D), F32),
            pltpu.SMEM((1,), jnp.int32),
            pltpu.VMEM((2, S, R), F32),
            pltpu.VMEM((2, S + 2 * R, R), F32),
            pltpu.VMEM((2, T, D), BF),
            dma((2,)), dma((12,)), dma((2,)), dma((2,)),
            dma, dma, dma, dma,
            dma((2, H, 2)), dma((2, H, 2)), dma((2, H, 2)), dma((2, H, 2)), dma((2, H, 2)), dma((2, H, 2)),
            dma, dma, dma, dma, dma, dma,
        ],
        compiler_params=pltpu.CompilerParams(
            collective_id=0, has_side_effects=True, vmem_limit_bytes=61 * 1024 * 1024
        ),
    )(
        filled, q, k, v, ck, cv, gain.reshape(1, D), vb, xg, cstate, cfilter, skip.reshape(1, D)
    )


def solution(mesh):
    Z, U = mesh.shape["ctx"] // 2, mesh.shape["uly"]
    rows = P(("ctx", "uly"), None)
    return jax.shard_map(
        functools.partial(body, Z, U),
        mesh=mesh,
        in_specs=(rows, rows, rows, P("ctx", "uly"), P("ctx", "uly"), P(), P(), rows, rows, P(), P(), P()),
        out_specs=rows,
        check_vma=False,
    )
```

```python
import functools
import math

import jax
import jax.numpy as jnp
from jax import lax
from jax.experimental import pallas as pl
from jax.experimental.pallas import tpu as pltpu
from jax.sharding import PartitionSpec as P

MESH = pl.DeviceIdType.MESH
DH = 128
FLAG_ROWS = 16
NEG = -1e30
BIG = 1e30
N_AT = 2
PIECES = 2
BF = jnp.bfloat16
F32 = jnp.float32


def nt(a, b):
    return lax.dot_general(a, b, (((1,), (1,)), ((), ())), preferred_element_type=F32)


def kernel(
    Z, U,
    filled_in, q, k, v, ck, cv, gain_in, vb_in, xg_in, cstate_in, cfilter_in, skip_in,
    out,
    qbuf, kvn, raw, ka, kb, va, vt_b, o_a, m_a, o_s, o_r, s_s, s_r, obuf, att, vb_old, ext,
    gain, vb, xg, cstate, cfilter, skip, taps, filled, s_1, s_2, kvs,
    own_sem, self_sem, x_send, x_recv, q_send, q_recv, n_send, n_recv,
    g_send, g_recv, r_send, r_recv, t_send, t_recv, b_send, b_recv, h_send, h_recv, e_send, e_recv,
):
    T, D = q.shape
    S = ck.shape[0]
    W = 2 * U
    R = U * T
    H = Z // 2
    c_i = lax.axis_index("ctx")
    u = lax.axis_index("uly")
    z, xl = c_i // 2, lax.rem(c_i, 2)
    me = xl * U + u
    head_col = pl.multiple_of((2 * u + xl) * DH, DH)
    scale = math.log2(math.e) / math.sqrt(DH)

    def peer(o):
        return (2 * z + o // U, lax.rem(o, U))

    def ring(d):
        return lax.rem(z + Z + d, Z)

    partner = (2 * z + 1 - xl, u)
    flat = c_i * U + u
    n_dev = 2 * Z * U
    after, before = lax.rem(flat + 1, n_dev), lax.rem(flat + n_dev - 1, n_dev)

    barrier = pltpu.get_barrier_semaphore()

    def greet(i, carry):
        pl.semaphore_signal(barrier, inc=1, device_id=peer(lax.rem(me + i, W)), device_id_type=MESH)
        return carry

    lax.fori_loop(1, W, greet, 0)
    for d in (1, -1):
        pl.semaphore_signal(barrier, inc=1, device_id=(2 * ring(d) + xl, u), device_id_type=MESH)
    pl.semaphore_signal(barrier, inc=1, device_id=(before // U, lax.rem(before, U)), device_id_type=MESH)

    @pl.when(me == 0)
    def _():
        def greet_old(i, carry):
            at = (2 * ring(-1) + i // U, lax.rem(i, U))
            pl.semaphore_signal(barrier, inc=1, device_id=at, device_id_type=MESH)
            return carry

        lax.fori_loop(0, W, greet_old, 0)

    my_rows = pl.ds(pl.multiple_of(me * T, T), T)
    mine = pl.multiple_of(xl * DH, DH)
    other = pl.multiple_of((1 - xl) * DH, DH)
    loads = [
        pltpu.make_async_copy(src.at[:, pl.ds(mine, DH)], raw.at[0, i], own_sem.at[i])
        for i, src in enumerate((ck, cv))
    ]
    for load in loads:
        load.start()
    own_cols = pl.ds(head_col, DH)
    selves = [
        pltpu.make_async_copy(q.at[:, own_cols], qbuf.at[z, my_rows], self_sem.at[0]),
        pltpu.make_async_copy(k.at[:, own_cols], kvn.at[0, my_rows], self_sem.at[1]),
        pltpu.make_async_copy(v.at[:, own_cols], kvn.at[1, my_rows], self_sem.at[2]),
    ] + [
        pltpu.make_async_copy(src, dst, self_sem.at[3 + i])
        for i, (src, dst) in enumerate(
            ((gain_in, gain), (vb_in, vb), (xg_in, xg), (cstate_in, cstate), (cfilter_in, cfilter), (skip_in, skip))
        )
    ]
    selves += [pltpu.make_async_copy(src, kvs.at[i], self_sem.at[10 + i]) for i, src in enumerate((k, v))]
    fill = pltpu.make_async_copy(filled_in, filled, self_sem.at[9])
    fill.start()
    for load in selves:
        load.start()
    pl.semaphore_wait(barrier, W + 3)


    def q_copy(o):
        ou, ox = lax.rem(o, U), o // U
        cols = pl.ds(pl.multiple_of((2 * ou + ox) * DH, DH), DH)
        return pltpu.make_async_remote_copy(
            q.at[:, cols], qbuf.at[z, my_rows], q_send, q_recv, device_id=peer(o), device_id_type=MESH
        )

    def n_copy(o):
        ou, ox = lax.rem(o, U), o // U
        cols = pl.ds(pl.multiple_of((2 * ou + ox) * DH, DH), DH)
        return pltpu.make_async_remote_copy(
            kvs.at[:, :, cols], kvn.at[:, my_rows], n_send, n_recv, device_id=peer(o), device_id_type=MESH
        )

    def send_q(i, carry):
        q_copy(lax.rem(me + lax.rem(i + U // 2 - 2, W - 1) + 1, W)).start()
        return carry

    def send_n(i, carry):
        n_copy(lax.rem(me + i, W)).start()
        return carry

    lax.fori_loop(1, W, send_q, 0)
    swaps = [
        pltpu.make_async_remote_copy(
            src.at[:, pl.ds(other, DH)], raw.at[1, i], x_send.at[i], x_recv.at[i],
            device_id=partner, device_id_type=MESH,
        )
        for i, src in enumerate((ck, cv))
    ]
    for swap in swaps:
        swap.start()
    halo = pltpu.make_async_remote_copy(
        vb_in.at[pl.ds(T - 8, 8)], vb_old, h_send, h_recv, device_id=(after // U, lax.rem(after, U)), device_id_type=MESH
    )
    halo.start()

    def split_store(dst, at, x):
        x = x * scale
        hi = x.astype(BF)
        dst[pl.ds(at, x.shape[0]), 0:DH] = hi
        dst[pl.ds(at, x.shape[0]), DH : 2 * DH] = (x - hi.astype(F32)).astype(BF)

    def prepare(which, chunk_ctx, kdst, vdst):
        limit = filled[0] - chunk_ctx * S
        rows = lax.broadcasted_iota(jnp.int32, (S, DH), 0)
        keys = raw[which, 0].astype(F32)
        first = keys[0:1]
        split_store(kdst, 0, jnp.where(rows < limit, keys, first))
        values = jnp.where(rows < limit, raw[which, 1].astype(F32), 0.0)
        vdst[0:DH, 0:S] = values.T.astype(BF)
        lane = lax.broadcasted_iota(jnp.int32, (FLAG_ROWS, S), 1)
        row = lax.broadcasted_iota(jnp.int32, (FLAG_ROWS, S), 0)
        vdst[DH : DH + FLAG_ROWS, 0:S] = jnp.where((row == 0) & (lane < limit), 1.0, 0.0).astype(BF)

    def prepare_new():
        split_store(kb, S, kvn[0].astype(F32))
        vt_b[0:DH, S : S + 2 * R] = kvn[1].astype(F32).T.astype(BF)
        row = lax.broadcasted_iota(jnp.int32, (FLAG_ROWS, 2 * R), 0)
        vt_b[DH : DH + FLAG_ROWS, S : S + 2 * R] = jnp.where(row == 0, 1.0, 0.0).astype(BF)

    fill.wait()
    for load in loads:
        load.wait()
    prepare(0, c_i, ka, va)
    for load in selves:
        load.wait()

    n_taps, n_groups = cfilter.shape
    f_1 = cfilter[...]
    f_hi = f_1.astype(BF)
    f_2 = f_1 - f_hi.astype(F32)
    f_mid = f_2.astype(BF)
    f_lo = (f_2 - f_mid.astype(F32)).astype(BF)
    wide = min(512, D)

    def spread(i, carry):
        cols = pl.ds(pl.multiple_of(i * wide, wide), wide)
        group = lax.broadcasted_iota(jnp.int32, (n_groups, wide), 0) * (D // n_groups)
        off = i * wide + lax.broadcasted_iota(jnp.int32, (n_groups, wide), 1) - group
        pick = jnp.where((off >= 0) & (off < D // n_groups), 1.0, 0.0).astype(BF)
        one = functools.partial(jnp.dot, preferred_element_type=F32)
        taps[:, cols] = one(f_hi, pick) + one(f_mid, pick) + one(f_lo, pick)
        return carry

    lax.fori_loop(0, D // wide, spread, 0)

    def twice(zq, half):
        x = qbuf[zq, pl.ds(pl.multiple_of(half * R, R), R), :]
        return jnp.concatenate([x, x], axis=1)

    def has_slots(chunk_ctx):
        return jnp.broadcast_to(filled[0] - chunk_ctx * S, (1, R)) > 0

    def first_scores(slot, zq, half):
        s_1[slot] = nt(ka[...], twice(zq, half))

    def first_part(slot, zq, half):
        s = s_1[slot]
        top = jnp.max(s, axis=0, keepdims=True)
        p = jnp.exp2(s - top).astype(BF)
        o_a[zq, half] = jnp.dot(va[...], p, preferred_element_type=F32)
        m_a[zq, half] = jnp.where(has_slots(c_i), top, NEG)

    def q_hop(way, dist, half, zq, piece):
        rows = pl.ds(pl.multiple_of(half * R + piece * (R // PIECES), R // PIECES), R // PIECES)
        return pltpu.make_async_remote_copy(
            qbuf.at[zq, rows], qbuf.at[zq, rows], g_send.at[way, dist, half, piece], g_recv.at[way, dist, half, piece],
            device_id=(2 * ring(1 - 2 * way) + xl, u), device_id_type=MESH,
        )

    everyone = pl.ds(0, (W - 1) * T)
    pltpu.make_async_copy(qbuf.at[z, everyone], qbuf.at[z, everyone], q_recv).wait()
    if H > 1:
        for i in (0, 1):
            for way in (0, 1):
                for piece in range(PIECES):
                    q_hop(way, 0, (way + i) % 2, z, piece).start()

    steps = 2 * Z

    def arrival(t):
        early, far = t < 2, t >= steps - 2
        j = lax.rem(t + 2, 4)
        way = jnp.where(early, 0, jnp.where(far, t - (steps - 2), lax.rem(j, 2)))
        half = jnp.where(early, t, jnp.where(far, t - (steps - 2), jnp.where(j < 2, lax.rem(j, 2), 1 - lax.rem(j, 2))))
        dist = jnp.where(early, 0, jnp.where(far, H, (t + 2) // 4))
        return way, half, dist, ring(dist * (2 * way - 1))

    def second_scores(slot, zq, half):
        s_2[slot] = nt(kb[...], twice(zq, half))

    def second_part(slot, zq, half):
        s = s_2[slot]
        s_c, s_n = s[0:S], s[S : S + 2 * R]
        key_at = z * (2 * R) + lax.broadcasted_iota(jnp.int32, (2 * R, R), 0)
        token_at = zq * (2 * R) + half * R + lax.broadcasted_iota(jnp.int32, (2 * R, R), 1)
        s_n = jnp.where(key_at <= token_at, s_n, NEG)
        filled_here = has_slots(2 * z + 1 - xl)
        top_c = jnp.where(filled_here, jnp.max(s_c, axis=0, keepdims=True), NEG)
        m_1 = m_a[zq, half]
        top = jnp.maximum(jnp.maximum(top_c, m_1), jnp.max(s_n, axis=0, keepdims=True))
        p_c = jnp.exp2(s_c - jnp.where(filled_here, top, BIG)).astype(BF)
        p_n = jnp.exp2(s_n - top).astype(BF)
        o = o_a[zq, half] * jnp.exp2(m_1 - top)
        o = o + jnp.dot(vt_b[...], jnp.concatenate([p_c, p_n], axis=0), preferred_element_type=F32)
        o_a[zq, half] = o
        m_a[zq, half] = top

    def arrive(t, slot):
        way, half, dist, zq = arrival(t)

        @pl.when(t >= 2)
        def _():
            for piece in range(PIECES):
                q_hop(way, dist - 1, half, zq, piece).wait_recv()

                @pl.when((dist < H - 1) | ((dist == H - 1) & (half == way)))
                def _():
                    q_hop(way, dist, half, zq, piece).start()

        first_scores(slot, zq, half)

    def weigh(t, slot):
        _, half, _, zq = arrival(t)
        first_part(slot, zq, half)

    def gather(begin, end):
        def pair(i, carry):
            t = begin + 2 * i
            arrive(t + 1, 1)
            weigh(t, 0)

            if begin == 0:
                @pl.when(i == min(N_AT, (end - begin) // 2 - 2))
                def _():
                    lax.fori_loop(1, W, send_n, 0)

            arrive(t + 2, 0)
            weigh(t + 1, 1)
            return carry

        arrive(jnp.int32(begin), 0)
        lax.fori_loop(0, (end - begin) // 2 - 1, pair, 0)
        arrive(jnp.int32(end - 1), 1)
        weigh(jnp.int32(end - 2), 0)
        weigh(jnp.int32(end - 1), 1)

    gather(0, steps - 2)
    for swap in swaps:
        swap.wait_recv()
    prepare(1, 2 * z + 1 - xl, kb, vt_b)
    pltpu.make_async_copy(kvn.at[:, everyone], kvn.at[:, everyone], n_recv).wait()
    prepare_new()

    def o_hop(way, slot, half, piece):
        rows = pl.ds(piece * (DH // PIECES), DH // PIECES)
        return pltpu.make_async_remote_copy(
            o_s.at[way, slot, half, rows], o_r.at[way, slot, half, rows], r_send.at[way, slot, half, piece],
            r_recv.at[way, slot, half, piece], device_id=(2 * ring(1 - 2 * way) + xl, u), device_id_type=MESH,
        )

    def s_hop(way, slot, half):
        return pltpu.make_async_remote_copy(
            s_s.at[way, slot, half], s_r.at[way, slot, half], t_send.at[way, slot, half],
            t_recv.at[way, slot, half], device_id=(2 * ring(1 - 2 * way) + xl, u), device_id_type=MESH,
        )

    def factors(zq, half, way, slot):
        s_hop(way, slot, half).wait_recv()
        m_1 = m_a[zq, half]
        m_2 = s_r[way, slot, half, 0:1]
        top = jnp.maximum(m_1, m_2)
        f_1, f_2 = jnp.exp2(m_1 - top), jnp.exp2(m_2 - top)
        m_a[zq, half] = top
        o_a[zq, half, DH : DH + 1] = o_a[zq, half, DH : DH + 1] * f_1 + s_r[way, slot, half, 1:2] * f_2
        return f_1, f_2

    def merge(zq, half, way, slot):
        f_1, f_2 = factors(zq, half, way, slot)
        for piece in range(PIECES):
            o_hop(way, slot, half, piece).wait_recv()
        o_a[zq, half, 0:DH] = o_a[zq, half, 0:DH] * f_1 + o_r[way, slot, half].astype(F32) * f_2

    def back(o):
        return pltpu.make_async_remote_copy(
            obuf.at[pl.ds(2 * o, 3)], att.at[:, :, own_cols], b_send, b_recv, device_id=peer(o), device_id_type=MESH
        )

    def back_first():
        return pltpu.make_async_remote_copy(
            obuf.at[pl.ds(1, 2)], att.at[pl.ds(1, 2), :, own_cols], b_send, b_recv, device_id=peer(0), device_id_type=MESH
        )

    edge = pltpu.make_async_remote_copy(
        obuf.at[pl.ds(2 * W, 1)], att.at[pl.ds(0, 1), :, own_cols], e_send, e_recv,
        device_id=(2 * ring(1), 0), device_id_type=MESH,
    )

    def departure(t):
        first, own = t < 2, t >= steps - 2
        j = lax.rem(t + 2, 4)
        half = jnp.where(first, t, jnp.where(own, t - (steps - 2), lax.rem(j, 2)))
        way = jnp.where(first, t, jnp.where(j < 2, 1 - lax.rem(j, 2), lax.rem(j, 2)))
        dist = jnp.where(first, H, jnp.where(own, 0, H - (t + 2) // 4))
        return way, half, dist, ring(dist * (1 - 2 * way))

    def score(t, slot):
        _, half, _, zq = departure(t)
        second_scores(slot, zq, half)

    def ship(t, slot):
        way, half, dist, zq = departure(t)
        own = t >= steps - 2
        second_part(slot, zq, half)

        @pl.when(jnp.logical_not(own))
        def _():
            out_slot = dist - 1

            def send_stats():
                s_s[way, out_slot, half, 0:1] = m_a[zq, half]
                s_s[way, out_slot, half, 1:2] = o_a[zq, half, DH : DH + 1]
                s_hop(way, out_slot, half).start()

            joins = (dist < H - 1) | ((dist == H - 1) & (half == way))

            @pl.when(joins)
            def _():
                f_1, f_2 = factors(zq, half, way, dist)
                send_stats()
                for piece in range(PIECES):
                    rows = slice(piece * (DH // PIECES), (piece + 1) * (DH // PIECES))
                    o_hop(way, dist, half, piece).wait_recv()
                    o_s[way, out_slot, half, rows] = (
                        o_a[zq, half, rows] * f_1 + o_r[way, dist, half, rows].astype(F32) * f_2
                    ).astype(BF)
                    o_hop(way, out_slot, half, piece).start()

            @pl.when(jnp.logical_not(joins))
            def _():
                send_stats()
                for piece in range(PIECES):
                    rows = slice(piece * (DH // PIECES), (piece + 1) * (DH // PIECES))
                    o_s[way, out_slot, half, rows] = o_a[zq, half, rows].astype(BF)
                    o_hop(way, out_slot, half, piece).start()

        @pl.when(own)
        def _():
            merge(z, half, 0, 0)
            merge(z, half, 1, 0)
            done = o_a[z, half, 0:DH] / o_a[z, half, DH : DH + 1]
            obuf[pl.ds(1 + half * (R // 8), R // 8)] = done.T.reshape(R // 8, 8, DH).astype(BF)

            def send_back(i, c):
                o = half * U + lax.rem(u + U // 2 + i, U)

                @pl.when((o != me) & (o > 0))
                def _():
                    back(o).start()

                @pl.when((o != me) & (o == 0))
                def _():
                    back_first().start()

                return c

            lax.fori_loop(0, U, send_back, 0)

    def scatter_pair(i, carry):
        score(2 * i + 1, 1)
        ship(2 * i, 0)
        score(jnp.minimum(2 * i + 2, steps - 1), 0)
        ship(2 * i + 1, 1)
        return carry

    for t in (0, 1):
        arrive(jnp.int32(steps - 2 + t), t)
        score(jnp.int32(t), t)
        weigh(jnp.int32(steps - 2 + t), t)
        ship(jnp.int32(t), t)
    score(jnp.int32(2), 0)
    lax.fori_loop(1, steps // 2, scatter_pair, 0)
    edge.start()

    @pl.when(me == 0)
    def _():
        att[1:3, :, own_cols] = obuf[1:3]

    @pl.when(me > 0)
    def _():
        att[:, :, own_cols] = obuf[pl.ds(2 * me, 3)]

    pltpu.make_async_copy(qbuf.at[z, everyone], qbuf.at[z, everyone], q_send).wait()
    pltpu.make_async_copy(kvn.at[:, everyone], kvn.at[:, everyone], n_send).wait()
    for swap in swaps:
        swap.wait_send()
    halo.wait()
    for way in (0, 1):
        for half in (0, 1):
            for d in range(H):
                if d < H - 1 or half == way:
                    for piece in range(PIECES):
                        q_hop(way, d, half, z, piece).wait_send()
                        o_hop(way, d, half, piece).wait_send()
                    s_hop(way, d, half).wait_send()

    def bytes_of(blocks, columns, sem):
        part = att.at[pl.ds(0, blocks), :, pl.ds(0, columns)]
        return pltpu.make_async_copy(part, part, sem)

    @pl.when(me == 0)
    def _():
        bytes_of(2, (W - 1) * DH, b_recv).wait()
        bytes_of(3, (W - 1) * DH, b_send).wait()
        bytes_of(1, W * DH, e_recv).wait()

    @pl.when(me > 0)
    def _():
        bytes_of(3, (W - 1) * DH, b_recv).wait()
        bytes_of(3, (W - 2) * DH, b_send).wait()
        bytes_of(2, DH, b_send).wait()

    edge.wait_send()

    for i in range(3):
        x = att[i].astype(F32)
        inv = lax.rsqrt(jnp.mean(x * x, axis=1, keepdims=True) + 1e-06)
        branch = vb_old[...] if i == 0 else vb[8 * (i - 1) : 8 * i]
        ext[8 * i : 8 * i + 8, :] = (x * inv * gain[...] * branch.astype(F32)).astype(BF).astype(F32)

    @pl.when(flat == 0)
    def _():
        ext[8 - cstate.shape[0] : 8, :] = cstate[...].astype(F32)

    total = taps[0:1] * ext[8 : 8 + T]
    for lag in range(1, n_taps):
        total = total + taps[lag : lag + 1] * ext[8 - lag : 8 - lag + T]
    out[...] = (xg[...].astype(F32) * (total + skip[...] * ext[8 : 8 + T])).astype(BF)


def body(Z, U, q, k, v, ck, cv, filled, gain, vb, xg, cstate, cfilter, skip):
    T, D = q.shape
    S = ck.shape[0]
    R = U * T
    H = Z // 2
    vmem = pl.BlockSpec(memory_space=pltpu.VMEM)
    hbm = pl.BlockSpec(memory_space=pltpu.HBM)
    dma = pltpu.SemaphoreType.DMA
    return pl.pallas_call(
        functools.partial(kernel, Z, U),
        out_shape=jax.ShapeDtypeStruct((T, D), BF),
        in_specs=[hbm] * 12,
        out_specs=vmem,
        scratch_shapes=[
            pltpu.VMEM((Z, 2 * R, DH), BF),
            pltpu.VMEM((2, 2 * R, DH), BF),
            pltpu.VMEM((2, 2, S, DH), BF),
            pltpu.VMEM((S, 2 * DH), BF),
            pltpu.VMEM((S + 2 * R, 2 * DH), BF),
            pltpu.VMEM((DH + FLAG_ROWS, S), BF),
            pltpu.VMEM((DH + FLAG_ROWS, S + 2 * R), BF),
            pltpu.VMEM((Z, 2, DH + FLAG_ROWS, R), F32),
            pltpu.VMEM((Z, 2, 1, R), F32),
            pltpu.VMEM((2, H, 2, DH, R), BF),
            pltpu.VMEM((2, H, 2, DH, R), BF),
            pltpu.VMEM((2, H, 2, 2, R), F32),
            pltpu.VMEM((2, H, 2, 2, R), F32),
            pltpu.VMEM((1 + 2 * R // 8, 8, DH), BF),
            pltpu.VMEM((3, 8, D), BF),
            pltpu.VMEM((8, D), BF),
            pltpu.VMEM((24, D), F32),
            pltpu.VMEM((1, D), F32),
            pltpu.VMEM((T, D), BF),
            pltpu.VMEM((T, D), BF),
            pltpu.VMEM(cstate.shape, BF),
            pltpu.VMEM(cfilter.shape, F32),
            pltpu.VMEM((1, D), F32),
            pltpu.VMEM((cfilter.shape[0], D), F32),
            pltpu.SMEM((1,), jnp.int32),
            pltpu.VMEM((2, S, R), F32),
            pltpu.VMEM((2, S + 2 * R, R), F32),
            pltpu.VMEM((2, T, D), BF),
            dma((2,)), dma((12,)), dma((2,)), dma((2,)),
            dma, dma, dma, dma,
            dma((2, H, 2, PIECES)), dma((2, H, 2, PIECES)), dma((2, H, 2, PIECES)), dma((2, H, 2, PIECES)),
            dma((2, H, 2)), dma((2, H, 2)),
            dma, dma, dma, dma, dma, dma,
        ],
        compiler_params=pltpu.CompilerParams(
            collective_id=0, has_side_effects=True, vmem_limit_bytes=61 * 1024 * 1024
        ),
    )(
        filled, q, k, v, ck, cv, gain.reshape(1, D), vb, xg, cstate, cfilter, skip.reshape(1, D)
    )


def solution(mesh):
    Z, U = mesh.shape["ctx"] // 2, mesh.shape["uly"]
    rows = P(("ctx", "uly"), None)
    return jax.shard_map(
        functools.partial(body, Z, U),
        mesh=mesh,
        in_specs=(rows, rows, rows, P("ctx", "uly"), P("ctx", "uly"), P(), P(), rows, rows, P(), P(), P()),
        out_specs=rows,
        check_vma=False,
    )
```
